32 devices in a mesh: seq: 8 (over z, x), mp: 4 (over y, core).
Axes of the slice: x: 2, y: 2, z: 4, core: 2. Of those that a mesh axis runs over, the one named last changes fastest.
Arguments:
- tokens: bfloat16 [4096, 2048], P('seq'), may hold values from -6 to 6
- cotangent: bfloat16 [4096, 2048], P('seq'), may hold values from -6 to 6
- w_query: bfloat16 [2048, 2048], P('seq', 'mp'), may hold values from -0.125 to 0.125
- w_key: bfloat16 [2048, 2048], P('seq', 'mp'), may hold values from -0.125 to 0.125
- w_value: bfloat16 [2048, 2048], P('seq', 'mp'), may hold values from -0.125 to 0.125
- w_output: bfloat16 [2048, 2048], P('mp', 'seq'), may hold values from -0.125 to 0.125
- carry_state: float32 [16, 128, 128], P('mp'), may hold values from -512 to 512
Outputs:
- grad_tokens: bfloat16 [4096, 2048], P('seq', 'mp')
- grad_query: float32 [2048, 2048], P('seq', 'mp')
- grad_key: float32 [2048, 2048], P('seq', 'mp')
- grad_value: float32 [2048, 2048], P('seq', 'mp')
- grad_output: float32 [2048, 2048], P('mp', 'seq')
The draws below stay inside these ranges and needn't reach their ends.
All inputs are finite; a program needn't handle non-finite values.
Results may differ from the reference program's by a relative error of at most 0.015.
Values may be sent and summed in bfloat16 or wider, within the bound.
No kernel may reach another device: no remote copies, remote signals or barrier semaphores. Data moves between devices by JAX's collectives and lax.ppermute only.
A program may use at most 128 MiB of HBM per device.

```python
import jax
import jax.numpy as jnp
from jax import lax

D = 2048
HEAD_DIM = 128
TOK_DEV = 512
HEADS = 16
HD = 2048
LEN = 4096
N_MP = 4


def with_spikes(array, key, source, target, blocks, factor):
    def block_of(dim):
        return (jnp.arange(array.shape[dim]) // (array.shape[dim] // blocks)).reshape((-1,) + (1,) * (array.ndim - 1 - dim))

    near = jax.random.permutation(key, blocks)[block_of(target)]
    second = (block_of(target) + blocks // 2) % blocks
    return jnp.where((block_of(source) == near) | (block_of(source) == second), factor * array, array)


def level_of(key, extent, cuts, low, largest):
    def one(dim, shards_of):
        draws = jax.random.uniform(jax.random.fold_in(jax.random.fold_in(key, 6), dim), (shards_of,), jnp.float32, low / len(cuts), largest / len(cuts))
        return jnp.repeat(jnp.exp(draws), extent[dim] // shards_of).reshape((-1,) + (1,) * (len(extent) - dim - 1))

    factor_of = one(*cuts[0])
    for cut in cuts[1:]:
        factor_of = factor_of * one(*cut)
    return factor_of


def centred(own_key, dims, deviation, bound, split=(), held_as=jnp.bfloat16):
    values = jax.random.normal(own_key, dims, jnp.float32) * deviation
    if len(split) > 0:
        values = level_of(own_key, dims, split, -0.22, 0.18) * values
    return jnp.clip(values, min=-bound, max=bound).astype(held_as)


def noise_with(rng, dims, deviation, limit, pieces, heavy, kind=jnp.bfloat16):
    values = deviation * jax.random.normal(rng, dims, jnp.float32)
    if pieces:
        values = values * level_of(rng, dims, pieces, -0.22, 0.18)
    return jnp.clip(with_spikes(values, jax.random.fold_in(rng, 3), *heavy), -limit, limit).astype(kind)


def setup_inputs(seed: int = 0) -> dict:
    key_of = jax.random.split(jax.random.key(seed), 8)
    return {
        "tokens": noise_with(key_of[0], (LEN, D), 1.0, 6.0, ((0, 8),), (0, 1, 8, 2.0)),
        "cotangent": centred(key_of[1], (LEN, D), 1.0, 6.0, ((0, 8),)),
        "w_query": centred(key_of[2], (D, HD), D ** -0.5, 0.125, ((0, 8), (1, 4))),
        "w_key": centred(key_of[3], (D, HD), D ** -0.5, 0.125, ((0, 8), (1, 4))),
        "w_value": centred(key_of[4], (D, HD), D ** -0.5, 0.125, ((0, 8), (1, 4))),
        "w_output": centred(key_of[5], (HD, D), HD ** -0.5, 0.125, ((0, 4), (1, 8))),
        "carry_state": centred(key_of[6], (HEADS, HEAD_DIM, HEAD_DIM), (4 * TOK_DEV ** 0.5), 512.0, ((0, 4),), jnp.float32),
    }


def reference(tokens, cotangent, w_query, w_key, w_value, w_output, carry_state):
    block_count = LEN // TOK_DEV
    highest = lax.Precision.HIGHEST

    def project(weight):
        result = jnp.dot(tokens, weight, preferred_element_type=jnp.float32).astype(jnp.bfloat16)
        return result.reshape(block_count, TOK_DEV, HEADS, HEAD_DIM)
    queries = project(w_query)
    keys_all = project(w_key)
    values_all = project(w_value)
    position = jnp.arange(TOK_DEV)
    causal = (position[:, None] >= position[None, :])[None]

    def forward_step(state, item):
        query_rows, key_rows, value_rows = item
        query_f = query_rows.astype(jnp.float32)
        key_f = key_rows.astype(jnp.float32)
        value_f = value_rows.astype(jnp.float32)
        scores = jnp.where(causal, jnp.einsum('thd,shd->hts', query_f, key_f), 0.0).astype(jnp.bfloat16)
        inner = jnp.einsum('hts,shd->thd', scores.astype(jnp.float32), value_f)
        outer = jnp.einsum('thd,hde->the', query_f, state, precision=highest)
        updated = state + jnp.einsum('shd,she->hde', key_f, value_f)
        return (updated, (inner + outer, state))
    start_state = carry_state.astype(jnp.float32)
    final_state, (mixed, prefix) = lax.scan(forward_step, start_state, (queries, keys_all, values_all))
    rms = jnp.sqrt(lax.optimization_barrier(jnp.mean(mixed * mixed, axis=-1, keepdims=True)) + 1e-06)
    normed = mixed / rms
    attended = normed.astype(jnp.bfloat16).reshape(LEN, HD)
    grad_attended = jnp.dot(cotangent, w_output.T, preferred_element_type=jnp.float32).astype(jnp.bfloat16)
    grad_output = jnp.dot(attended.T, cotangent, preferred_element_type=jnp.float32)
    grad_normed = grad_attended.astype(jnp.float32).reshape(block_count, TOK_DEV, HEADS, HEAD_DIM)
    grad_mixed = ((grad_normed - normed * lax.optimization_barrier(jnp.mean(grad_normed * normed, axis=-1, keepdims=True))) / rms).astype(jnp.bfloat16)

    def backward_step(carried, item):
        query_rows, key_rows, value_rows, grad_rows, prefix_state = item
        query_f = query_rows.astype(jnp.float32)
        key_f = key_rows.astype(jnp.float32)
        value_f = value_rows.astype(jnp.float32)
        grad_f = grad_rows.astype(jnp.float32)
        scores = jnp.where(causal, jnp.einsum('thd,shd->hts', query_f, key_f), 0.0).astype(jnp.bfloat16).astype(jnp.float32)
        grad_scores = jnp.where(causal, jnp.einsum('the,she->hts', grad_f, value_f), 0.0).astype(jnp.bfloat16).astype(jnp.float32)
        grad_q = jnp.einsum('hts,shd->thd', grad_scores, key_f) + jnp.einsum('the,hde->thd', grad_f, prefix_state, precision=highest)
        grad_k = jnp.einsum('hts,thd->shd', grad_scores, query_f) + jnp.einsum('she,hde->shd', value_f, carried, precision=highest)
        grad_v = jnp.einsum('hts,the->she', scores, grad_f) + jnp.einsum('shd,hde->she', key_f, carried, precision=highest)
        updated = carried + jnp.einsum('thd,the->hde', query_f, grad_f)
        return (updated, (grad_q.astype(jnp.bfloat16), grad_k.astype(jnp.bfloat16), grad_v.astype(jnp.bfloat16)))
    zero_state = jnp.zeros((HEADS, HEAD_DIM, HEAD_DIM), jnp.float32)
    final_grad, (grad_queries, grad_keys, grad_values) = lax.scan(backward_step, zero_state, (queries, keys_all, values_all, grad_mixed, prefix), reverse=True)
    grad_queries = grad_queries.reshape(LEN, HD)
    grad_keys = grad_keys.reshape(LEN, HD)
    grad_values = grad_values.reshape(LEN, HD)
    grad_query = jnp.dot(tokens.T, grad_queries, preferred_element_type=jnp.float32)
    grad_key = jnp.dot(tokens.T, grad_keys, preferred_element_type=jnp.float32)
    grad_value = jnp.dot(tokens.T, grad_values, preferred_element_type=jnp.float32)
    group_width = HD // N_MP
    total = jnp.zeros((LEN, D), jnp.float32)
    for group in range(N_MP):
        lower = group * group_width
        upper = lower + group_width
        partial_sum = jnp.dot(grad_queries[:, lower:upper], w_query[:, lower:upper].T, preferred_element_type=jnp.float32)
        partial_sum = partial_sum + jnp.dot(grad_keys[:, lower:upper], w_key[:, lower:upper].T, preferred_element_type=jnp.float32)
        partial_sum = partial_sum + jnp.dot(grad_values[:, lower:upper], w_value[:, lower:upper].T, preferred_element_type=jnp.float32)
        rounded = lax.optimization_barrier(partial_sum.astype(jnp.bfloat16))
        total = total + rounded.astype(jnp.float32)
    return (total.astype(jnp.bfloat16), grad_query, grad_key, grad_value, grad_output)
```

```python
import jax
import jax.numpy as jnp
from jax import lax
from jax.experimental import pallas as pl
from jax.experimental.pallas import tpu as pltpu
from jax.sharding import PartitionSpec as P

HEAD_DIM = 128
PAIR = 2
BF = jnp.bfloat16
F32 = jnp.float32


def dot(left, right, contract):
    return lax.dot_general(left, right, ((contract[0], contract[1]), ((), ())), preferred_element_type=F32)


def mm(left, right):
    return dot(left, right, ((1,), (0,)))


def mm_rows(left, right):
    return dot(left, right, ((0,), (0,)))


def mm_cols(left, right):
    return dot(left, right, ((1,), (1,)))


def swap(array, axis, bit):
    return lax.ppermute(array, axis, [(i, i ^ bit) for i in range(lax.axis_size(axis))])


def pick(array, index, dim):
    return lax.dynamic_index_in_dim(array, index, dim, False)


def ordered(own, other, bit, dim):
    first = jnp.where(bit == 0, own, other)
    second = jnp.where(bit == 0, other, own)
    return jnp.stack([first, second], axis=dim)


def split_state(state):
    high = state.astype(BF)
    return high, (state - high.astype(F32)).astype(BF)


def state_kernel(key_ref, value_ref, out_ref):
    out_ref[0, 0] = mm_rows(key_ref[0], value_ref[0])


def core_kernel(q_ref, k_ref, v_ref, ga_ref, p_ref, att_ref, u_ref, gq_ref, gk_ref, gv_ref):
    q, k, v = q_ref[0], k_ref[0], v_ref[0]
    rows = q.shape[0]
    causal = lax.broadcasted_iota(jnp.int32, (rows, rows), 0) >= lax.broadcasted_iota(jnp.int32, (rows, rows), 1)
    p_high, p_low = split_state(p_ref[0, 0])
    scores = jnp.where(causal, mm_cols(q, k), 0.0).astype(BF)
    mixed = mm(scores, v) + mm(q, p_high) + mm(q, p_low)
    inverse = 1.0 / jnp.sqrt(jnp.mean(mixed * mixed, axis=-1, keepdims=True) + 1e-06)
    normed = mixed * inverse
    att_ref[0] = normed.astype(BF)
    grad = ga_ref[0].astype(F32)
    gm = ((grad - normed * jnp.mean(grad * normed, axis=-1, keepdims=True)) * inverse).astype(BF)
    u_ref[0, 0] = mm_rows(q, gm)
    gs = jnp.where(causal, mm_cols(gm, v), 0.0).astype(BF)
    gq_ref[0] = (mm(gs, k) + mm_cols(gm, p_high) + mm_cols(gm, p_low)).astype(BF)
    gk_ref[0] = mm_rows(gs, q)
    gv_ref[0] = mm_rows(scores, gm)


def finish_kernel(k_ref, v_ref, s_ref, gk_ref, gv_ref, gk_out, gv_out):
    s_high, s_low = split_state(s_ref[0, 0])
    gk_out[0] = (gk_ref[0] + mm_cols(v_ref[0], s_high) + mm_cols(v_ref[0], s_low)).astype(BF)
    gv_out[0] = (gv_ref[0] + mm(k_ref[0], s_high) + mm(k_ref[0], s_low)).astype(BF)


def on_heads(kernel, operands, outs, name, flops):
    blocks, rows, width = operands[0].shape
    row_spec = pl.BlockSpec((1, rows, HEAD_DIM), lambda b, h: (b, 0, h))
    state_spec = pl.BlockSpec((1, 1, HEAD_DIM, HEAD_DIM), lambda b, h: (b, h, 0, 0))
    spec_of = lambda array: row_spec if len(array.shape) == 3 else state_spec
    size = sum(a.size * a.dtype.itemsize for a in (*operands, *outs))
    return pl.pallas_call(
        kernel,
        grid=(blocks, width // HEAD_DIM),
        in_specs=[spec_of(a) for a in operands],
        out_specs=[spec_of(a) for a in outs],
        out_shape=outs,
        name=name,
        cost_estimate=pl.CostEstimate(flops=flops, bytes_accessed=size, transcendentals=0),
    )(*operands)


def per_device(tokens, cotangent, w_query, w_key, w_value, w_output, carry_state):
    count, groups = lax.axis_size("seq"), lax.axis_size("mp")
    place, group = lax.axis_index("seq"), lax.axis_index("mp")
    x = place & 1
    half = (place // PAIR) & 1
    far_bits = [1 << b for b in range(2, count.bit_length() - 1)]
    mp_bits = [1 << b for b in range(groups.bit_length() - 1)]
    rows, model = tokens.shape
    shard = w_query.shape[0]
    width = w_query.shape[1] // 2
    heads = width // HEAD_DIM

    def far(bit):
        return (place // bit) & 1

    def halves(array):
        split = array.reshape(rows, count // 2, 2, shard)
        return jnp.stack([pick(split, x, 2), pick(split, 1 - x, 2)]).reshape(2, rows, model // 2)

    def both_blocks(array):
        own = halves(array)
        part = rows // groups
        piece = lax.dynamic_slice_in_dim(own, group * part, part, 1)
        piece = swap(piece, "seq", PAIR)
        for i, bit in enumerate(reversed(mp_bits)):
            piece = ordered(piece, swap(piece, "mp", bit), (group // bit) & 1, 1 + i)
        other = piece.reshape(2, rows, model // 2)
        return jnp.concatenate([own, other], axis=1)

    stacked = jnp.stack([w_key, w_value, w_query, w_output.T]).reshape(4, shard, 2, width)
    given = swap(pick(stacked, 1 - half, 2), "seq", PAIR)
    paired = ordered(pick(stacked, half, 2), given, half, 1)

    def gather(block):
        for bit in far_bits:
            block = ordered(block, swap(block, "seq", bit), far(bit), 1)
            block = block.reshape(block.shape[0], -1, shard, width)
        return block.reshape(block.shape[0], -1, width), swap(block, "seq", 1).reshape(block.shape[0], -1, width)

    kv_own, kv_other = gather(paired[:2])
    toks = both_blocks(tokens)
    qo_own, qo_other = gather(paired[2:])
    cots = both_blocks(cotangent)

    def project(rows_of, own, other):
        return (mm(rows_of[0], own) + mm(rows_of[1], other)).astype(BF).reshape(2, rows, width)

    keys = project(toks, kv_own[0], kv_other[0])
    values = project(toks, kv_own[1], kv_other[1])
    cell = 2 * rows * HEAD_DIM * HEAD_DIM
    (state,) = on_heads(
        state_kernel, (keys, values), [jax.ShapeDtypeStruct((2, heads, HEAD_DIM, HEAD_DIM), F32)], "state", 2 * heads * cell
    )

    def scan(term, backward):
        def past(bit_of):
            return (1 - bit_of if backward else bit_of).astype(F32)

        got = swap(term.astype(BF), "seq", 1).astype(F32)
        total = term + got
        before = got * past(x)
        both = total[0] + total[1]
        before = before + jnp.stack([total[1] * past(half), total[0] * past(1 - half)])
        for bit in far_bits:
            got = swap(both.astype(BF), "seq", bit).astype(F32)
            before = before + (got * past(far(bit)))[None]
            both = both + got
        return before

    carry = lax.dynamic_slice_in_dim(carry_state, half * heads, heads, 0)
    prefix = carry[None] + scan(state, False)
    queries = project(toks, qo_own[0], qo_other[0])
    grad_att = project(cots, qo_own[1], qo_other[1])

    like = jax.ShapeDtypeStruct((2, rows, width), BF)
    wide = jax.ShapeDtypeStruct((2, rows, width), F32)
    product = 2 * rows * rows * HEAD_DIM
    attended, term, grad_q, part_k, part_v = on_heads(
        core_kernel,
        (queries, keys, values, grad_att, prefix),
        [like, jax.ShapeDtypeStruct((2, heads, HEAD_DIM, HEAD_DIM), F32), like, wide, wide],
        "core",
        2 * heads * (6 * product + 5 * cell),
    )

    def reduce_rows(rows_of, grads):
        send = jnp.stack([mm_rows(rows_of[1], g).astype(BF) for g in grads])
        keep = jnp.stack([mm_rows(rows_of[0], g) for g in grads])
        total = (keep + swap(send, "seq", 1).astype(F32)).reshape(len(grads), -1, shard, width)
        for bit in reversed(far_bits):
            total = total.reshape(len(grads), 2, -1, shard, width)
            got = swap(pick(total, 1 - far(bit), 1).astype(BF), "seq", bit)
            total = pick(total, far(bit), 1) + got.astype(F32)
        got = swap(pick(total, 1 - half, 1).astype(BF), "seq", PAIR)
        own = pick(total, half, 1)
        return ordered(own, got.astype(F32), half, 2).reshape(len(grads), shard, 2 * width)

    def flat(array):
        return array.reshape(2 * rows, width)

    grad_output = reduce_rows(cots, [flat(attended)])[0].T
    suffix = scan(term, True)
    grad_query = reduce_rows(toks, [flat(grad_q)])[0]
    grad_k, grad_v = on_heads(
        finish_kernel, (keys, values, suffix, part_k, part_v), [like, like], "finish", 2 * heads * 4 * cell
    )
    grad_key, grad_value = reduce_rows(toks, [flat(grad_k), flat(grad_v)])

    rest = model // 2 // groups
    core = (group & 1)

    def partial(index):
        total = None
        for grad, own, other in ((grad_q, qo_own[0], qo_other[0]), (grad_k, kv_own[0], kv_other[0]), (grad_v, kv_own[1], kv_other[1])):
            weight = pick(jnp.stack([own, other]).reshape(2, groups // 2, 2, rest, width), index, 2).reshape(-1, width)
            one = mm_cols(flat(grad), weight)
            total = one if total is None else total + one
        return total

    sent = partial(1 - core).astype(BF)
    total = partial(core) + swap(sent, "mp", 1).astype(F32)
    total = total.reshape(2, rows, model // 2)
    total = total[0] + swap(total[1].astype(BF), "seq", PAIR).astype(F32)
    total = total.reshape(rows, 2, groups // 2, rest)
    for bit in reversed(mp_bits[1:]):
        mine = (group // bit) & 1
        total = total.reshape(rows, 2, 2, -1, rest)
        got = swap(pick(total, 1 - mine, 2).astype(BF), "mp", bit)
        total = pick(total, mine, 2) + got.astype(F32)
    total = total.reshape(rows, 2, rest // shard, shard)
    total = ordered(total[:, 0], total[:, 1], x, 2)
    grad_tokens = total.reshape(rows, 2 * rest).astype(BF)
    return (grad_tokens, grad_query, grad_key, grad_value, grad_output)


def solution(mesh):
    in_specs = (
        P("seq", None),
        P("seq", None),
        P("seq", "mp"),
        P("seq", "mp"),
        P("seq", "mp"),
        P("mp", "seq"),
        P("mp", None, None),
    )
    out_specs = (P("seq", "mp"), P("seq", "mp"), P("seq", "mp"), P("seq", "mp"), P("mp", "seq"))
    return jax.shard_map(
        per_device, mesh=mesh, in_specs=in_specs, out_specs=out_specs, check_vma=False
    )
```
